32 devices in a mesh: grp: 2 (over y), pair: 4 (over z), aux: 2 (over x), rep: 2 (over core).
Axes of the slice: x: 2, y: 2, z: 4, core: 2. Of those that a mesh axis runs over, the one named last changes fastest.
Arguments:
- three_center: bfloat16 [5120, 4, 8000], P(('grp', 'aux', 'rep', 'pair')), parts along dimension 0, may hold values from -0.050591038 to 0.050591038
- eps_occ: float32 [8], P('grp'), parts along dimension 0, may hold values from -1.2 to -0.4
- eps_virt: float32 [16000], P(('grp', 'pair')), parts along dimension 0, may hold values from 0.2 to 3
- freq: float32 [2], P('grp'), parts along dimension 0, may hold values from 0.2 to 2
Outputs:
- polar: float32 [5120, 2560], P(('grp', 'aux', 'rep'), 'pair'), parts along dimension 0
The draws below stay inside these ranges and needn't reach their ends.
There are 2 independent parts, one for each index of `grp`. The reference program is written for one: setup_inputs(seed, part) draws one part's arguments, and reference() takes and returns one part's arrays. A program takes and returns all parts, laid end to end along the dimension named above; each array names one. Nothing has to cross between parts.
All inputs are finite; a program needn't handle non-finite values.
Results may differ from the reference program's by a relative error of at most 0.0003.
Values may be sent and summed in bfloat16 or wider, within the bound.
A program may use at most 192 MiB of HBM per device.

```python
import math
import jax
import jax.numpy as jnp
from jax import lax

NAUX = 2560
NVIRT = 8000
NOCC = 4


def draw_three_center(key, part):
    key_factors, key_basis, key_noise = jax.random.split(key, 3)
    width = NOCC * NVIRT
    factor_count = 16
    scale = 1.5 * width ** (-0.5)
    factors = jax.random.normal(key_factors, (NAUX, factor_count), jnp.float32)
    basis = jax.random.normal(key_basis, (factor_count, width), jnp.float32)
    shared = jnp.dot(factors, basis, precision=lax.Precision.HIGHEST) * factor_count ** (-0.5)
    noise = jax.random.normal(key_noise, (NAUX, width), jnp.float32)
    mixed = 0.5 * noise + 0.866 * shared
    mixed = jnp.clip(mixed, -6.0, 6.0)
    return (scale * mixed).reshape(NAUX, NOCC, NVIRT).astype(jnp.bfloat16)


def levels(own_key, dims, pieces, smallest, top_value):
    loudness, own = 1.0, jax.random.fold_in(own_key, 6)
    for position, blocks in pieces:
        steps = jnp.exp(jax.random.uniform(jax.random.fold_in(own, position), (blocks,), jnp.float32, smallest / len(pieces), top_value / len(pieces)))
        loudness = loudness * jnp.repeat(steps, dims[position] // blocks).reshape([-1 if axis == position else 1 for axis in range(len(dims))])
    return loudness


def setup_inputs(seed: int = 0, part: int = 0) -> dict:
    key_of = jax.random.split(jax.random.key(seed), 5)
    part_keys = jax.random.split(jax.random.fold_in(key_of[4], part), 5)
    three_center = draw_three_center(jax.random.fold_in(jax.random.fold_in(key_of[4], part), 71), part)
    eps_occ = jnp.clip(jax.random.uniform(part_keys[1], (NOCC,), jnp.float32, -1.2, -0.4), -1.2, -0.4)
    eps_virt = jnp.clip(0.2 + 2.8 * jax.random.uniform(part_keys[2], (NVIRT,), jnp.float32) ** levels(part_keys[2], (NVIRT,), ((0, 4),), -0.2, 0.2), 0.2, 3.0)
    freq = jnp.clip(jnp.exp(jax.random.uniform(part_keys[3], (1,), jnp.float32, math.log(0.2), math.log(2.0))), 0.2, 2.0)
    return dict(three_center=three_center, eps_occ=eps_occ, eps_virt=eps_virt, freq=freq)


def reference(three_center, eps_occ, eps_virt, freq):
    excite = eps_virt[None, :] - eps_occ[:, None]
    weight = 2.0 * excite / (excite * excite + freq[0] * freq[0])
    scaled = (three_center.astype(jnp.float32) * weight[None, :, :]).astype(jnp.bfloat16)
    left = scaled.reshape(NAUX, NOCC * NVIRT)
    right = three_center.reshape(NAUX, NOCC * NVIRT)
    blocks = left.reshape(8, NAUX // 8, NOCC * NVIRT)

    def one_block(rows):
        return lax.dot_general(rows, right, (((1,), (1,)), ((), ())), preferred_element_type=jnp.float32)

    return lax.map(one_block, blocks).reshape(NAUX, NAUX)
```

```python
import functools
import jax
import jax.numpy as jnp
from jax import lax
from jax.experimental import pallas as pl
from jax.experimental.pallas import tpu as pltpu
from jax.sharding import PartitionSpec as P

MESH = pl.DeviceIdType.MESH


def gather_kernel(sizes, x_ref, g_ref, zs, zr, xs, xr, cs, cr, ls):
    n_pair, n_aux, n_rep, chunks, rows = sizes
    z = lax.axis_index("pair")
    a = lax.axis_index("aux")
    r = lax.axis_index("rep")
    step = rows // chunks

    def turn(i, k, n):
        return lax.rem(i + k, n)

    peers = (
        [("pair", turn(z, k, n_pair)) for k in range(1, n_pair)]
        + [("aux", turn(a, k, n_aux)) for k in range(1, n_aux)]
        + [("rep", turn(r, k, n_rep)) for k in range(1, n_rep)]
    )
    barrier = pltpu.get_barrier_semaphore()
    for name, index in peers:
        pl.semaphore_signal(barrier, inc=1, device_id={name: index}, device_id_type=MESH)
    pl.semaphore_wait(barrier, len(peers))

    def block(aux, rep, pair, c):
        return g_ref.at[aux, rep, pair, pl.ds(c * step, step)]

    def z_copy(c, k, sending):
        to = turn(z, k, n_pair)
        src = turn(z, n_pair - k, n_pair)
        return pltpu.make_async_remote_copy(
            src_ref=x_ref.at[to, pl.ds(c * step, step)],
            dst_ref=block(a, r, z if sending else src, c),
            send_sem=zs.at[c, k],
            recv_sem=zr.at[c, k],
            device_id={"pair": to},
            device_id_type=MESH,
        )

    def x_copy(c, k, j, sending):
        pair = turn(z, n_pair - j, n_pair)
        mine = a if sending else turn(a, n_aux - k, n_aux)
        if j == 0 and sending:
            src = x_ref.at[z, pl.ds(c * step, step)]
        else:
            src = block(mine, r, pair, c)
        return pltpu.make_async_remote_copy(
            src_ref=src,
            dst_ref=block(mine, r, pair, c),
            send_sem=xs.at[c, k, j],
            recv_sem=xr.at[c, k, j],
            device_id={"aux": turn(a, k, n_aux)},
            device_id_type=MESH,
        )

    def c_copy(c, m, k, j, sending):
        pair = turn(z, n_pair - j, n_pair)
        aux = turn(a, n_aux - k, n_aux)
        rep = r if sending else turn(r, n_rep - m, n_rep)
        if j == 0 and k == 0 and sending:
            src = x_ref.at[z, pl.ds(c * step, step)]
        else:
            src = block(aux, rep, pair, c)
        return pltpu.make_async_remote_copy(
            src_ref=src,
            dst_ref=block(aux, rep, pair, c),
            send_sem=cs.at[c, m, k, j],
            recv_sem=cr.at[c, m, k, j],
            device_id={"rep": turn(r, m, n_rep)},
            device_id_type=MESH,
        )

    for c in range(chunks):
        for k in range(1, n_pair):
            z_copy(c, k, True).start()
    own = pltpu.make_async_copy(x_ref.at[z], g_ref.at[a, r, z], ls)
    own.start()

    def arrived(c, j):
        if j:
            z_copy(c, j, False).wait_recv()
        for k in range(1, n_aux):
            x_copy(c, k, j, True).start()
        for m in range(1, n_rep):
            c_copy(c, m, 0, j, True).start()

    def crossed(c, j):
        for k in range(1, n_aux):
            x_copy(c, k, j, False).wait_recv()
            for m in range(1, n_rep):
                c_copy(c, m, k, j, True).start()

    for c in range(chunks):
        arrived(c, 0)
    for c in range(chunks):
        for j in range(1, n_pair):
            arrived(c, j)
        crossed(c, 0)
        if c:
            for j in range(1, n_pair):
                crossed(c - 1, j)
    for j in range(1, n_pair):
        crossed(chunks - 1, j)

    own.wait()
    for c in range(chunks):
        for k in range(1, n_pair):
            z_copy(c, k, True).wait_send()
        for j in range(n_pair):
            for k in range(1, n_aux):
                x_copy(c, k, j, True).wait_send()
            for m in range(1, n_rep):
                for k in range(n_aux):
                    c_copy(c, m, k, j, True).wait_send()
                    c_copy(c, m, k, j, False).wait_recv()


def gather(pieces, n_aux, n_rep):
    n_pair, rows, width = pieces.shape
    chunks = 5 if rows % 80 == 0 else 1
    sizes = (n_pair, n_aux, n_rep, chunks, rows)
    dma = pltpu.SemaphoreType.DMA
    return pl.pallas_call(
        functools.partial(gather_kernel, sizes),
        out_shape=jax.ShapeDtypeStruct((n_aux, n_rep, n_pair, rows, width), pieces.dtype),
        in_specs=[pl.BlockSpec(memory_space=pl.ANY)],
        out_specs=pl.BlockSpec(memory_space=pl.ANY),
        scratch_shapes=[
            dma((chunks, n_pair)),
            dma((chunks, n_pair)),
            dma((chunks, n_aux, n_pair)),
            dma((chunks, n_aux, n_pair)),
            dma((chunks, n_rep, n_aux, n_pair)),
            dma((chunks, n_rep, n_aux, n_pair)),
            dma,
        ],
        compiler_params=pltpu.CompilerParams(collective_id=0, has_side_effects=True),
    )(pieces)


def encode(y):
    top = jnp.maximum(jnp.max(jnp.abs(y), axis=0, keepdims=True), 1e-30)
    scales = jnp.broadcast_to(top, (16, top.shape[1])).astype(jnp.bfloat16)
    power = jnp.abs(y) * (180.0 / scales[:1].astype(jnp.float32))
    for _ in range(4):
        power = power * power
    return jnp.where(y < 0, -power, power).astype(jnp.bfloat16), scales


def decode(code, scales):
    power = code.astype(jnp.float32)
    size = jnp.abs(power)
    root = jnp.maximum(size, 1e-37)
    for _ in range(4):
        root = lax.rsqrt(root)
    scale = scales[:1].astype(jnp.float32) * (1.0 / 180.0)
    return jnp.where(size < 1e-37, 0.0, jnp.where(power < 0, -root, root)) * scale


def fused_kernel(
    sizes, x_ref, occ_ref, virt_ref, freq_ref, o_ref, g, own, p, n_out, n_in, f_out, f_in, s_out, s_in,
    levels, w_ref, zs, zr, xs, xr, cs, cr, ls, ns, nr, fs, fr, ss, sr, es, er,
):
    chunks, step, width, slots, ahead, lead = sizes
    z = lax.axis_index("pair")
    a = lax.axis_index("aux")
    r = lax.axis_index("rep")
    mine = 2 * a + r
    tall = 4 * step
    half = 2 * step
    flips = [z, z + 1 - 2 * lax.rem(z, 2), lax.rem(z + 2, 4), 3 - z]
    mirror = {"pair": mine, "aux": lax.div(z, 2), "rep": lax.rem(z, 2)}

    barrier = pltpu.get_barrier_semaphore()
    peers = [{"pair": flips[j]} for j in (1, 2, 3)] + [{"aux": 1 - a}, {"rep": 1 - r}]
    for peer in peers:
        pl.semaphore_signal(barrier, inc=1, device_id=peer, device_id_type=MESH)

    @pl.when(z != mine)
    def _():
        pl.semaphore_signal(barrier, inc=1, device_id=mirror, device_id_type=MESH)
        pl.semaphore_wait(barrier, len(peers) + 1)

    @pl.when(z == mine)
    def _():
        pl.semaphore_wait(barrier, len(peers))

    def send(src, dst, send_sem, recv_sem, to):
        return pltpu.make_async_remote_copy(
            src_ref=src, dst_ref=dst, send_sem=send_sem, recv_sem=recv_sem,
            device_id=to, device_id_type=MESH,
        )

    def z_copy(c, j, sending):
        dst = g.at[c, mine, z if sending else flips[j]]
        return send(x_ref.at[flips[j], c], dst, zs.at[c, j - 1], zr.at[c, j - 1], {"pair": flips[j]})

    def x_copy(c, j, sending):
        dst = g.at[c, 2 * (a if sending else 1 - a) + r, flips[j]]
        src = x_ref.at[z, c] if j == 0 and sending else dst
        return send(src, dst, xs.at[c, j], xr.at[c, j], {"aux": 1 - a})

    def c_copy(c, k, j, sending):
        aux = 1 - a if k else a
        dst = g.at[c, 2 * aux + (r if sending else 1 - r), flips[j]]
        src = x_ref.at[z, c] if j == 0 and k == 0 and sending else dst
        return send(src, dst, cs.at[c, k, j], cr.at[c, k, j], {"rep": 1 - r})

    def e_copy(j, sending):
        dst = levels.at[z if sending else flips[j]]
        return send(virt_ref, dst, es.at[j - 1], er.at[j - 1], {"pair": flips[j]})

    def span(c, unit):
        begin = unit * c * (c + 1) // 2 + 16 * c
        return begin, unit * (c + 1)

    def both(begin, size):
        return pl.ds(begin, size + 16)

    def near(c):
        rows = both(*span(c, tall))
        return send(n_out.at[rows], n_in.at[rows], ns.at[c], nr.at[c], {"pair": flips[1]})

    def far(c):
        rows = both(*span(c, half))
        return send(f_out.at[rows], f_in.at[rows], fs.at[c], fr.at[c], {"pair": flips[2]})

    def swap(c):
        rows = both(*span(c - 1, half))
        return send(s_out.at[rows], s_in.at[rows], ss.at[c], sr.at[c], mirror)

    def write(ref, where, y):
        begin, size = where
        ref[begin : begin + size], ref[begin + size : begin + size + 16] = encode(y)

    def read(ref, where):
        begin, size = where
        return decode(ref[begin : begin + size], ref[begin + size : begin + size + 16])

    def low(shape):
        return lax.broadcasted_iota(jnp.int32, shape, 1) < tall

    def start_z(c):
        if c < chunks:
            for j in (1, 2, 3):
                z_copy(c, j, True).start()

    def start_own(c):
        if c < chunks:
            x_copy(c, 0, True).start()
            c_copy(c, 0, 0, True).start()

    def arrive(c, j):
        z_copy(c, j, False).wait_recv()
        x_copy(c, j, True).start()
        c_copy(c, 0, j, True).start()

    def weigh():
        levels[z] = virt_ref[...]
        for j in (1, 2, 3):
            e_copy(j, False).wait_recv()
        freq = freq_ref[0]
        piece = virt_ref.shape[1]
        for k in range(4):
            excite = levels[k] - occ_ref[z]
            w_ref[:, k * piece : (k + 1) * piece] = 2.0 * excite / (excite * excite + freq * freq)

    def scale(c):
        plain = g[c, mine].reshape(tall, width).astype(jnp.float32)
        own[c * tall : (c + 1) * tall] = (plain * w_ref[...]).astype(jnp.bfloat16)

    def cross(c):
        for j in range(4):
            x_copy(c, j, False).wait_recv()
            c_copy(c, 1, j, True).start()
        for j in range(4):
            for k in range(2):
                c_copy(c, k, j, False).wait_recv()

    def compute(c):
        rows = (c + 1) * tall
        rhs = jnp.concatenate([g[c, flips[j]].reshape(tall, width) for j in (0, 2, 1, 3)], axis=0)
        p[c % slots, :rows] = lax.dot_general(
            own[:rows], rhs, (((1,), (1,)), ((), ())), preferred_element_type=jnp.float32
        )
        write(n_out, span(c, tall), p[c % slots, :rows, 2 * tall :])
        near(c).start()

    def nearer(c):
        rows = (c + 1) * tall
        near(c).wait_recv()
        p[c % slots, :rows, : 2 * tall] += read(n_in, span(c, tall))
        upper = p[c % slots, : rows // 2, : 2 * tall]
        lower = p[c % slots, rows // 2 : rows, : 2 * tall]
        folded = jnp.where(low(upper.shape), pltpu.roll(upper, tall, 1), lower)
        write(f_out, span(c, half), folded)
        far(c).start()

    def finish(c):
        rows = (c + 1) * tall
        far(c).wait_recv()
        got = read(f_in, span(c, half))
        p[c % slots, : rows // 2, : 2 * tall] += got
        p[c % slots, rows // 2 : rows, : 2 * tall] += pltpu.roll(got, tall, 1)
        if c:
            kept = c * half
            upper = p[c % slots, :kept, : 2 * tall]
            lower = p[c % slots, kept : 2 * kept, : 2 * tall]
            folded = jnp.where(low(upper.shape), upper, pltpu.roll(lower, tall, 1))
            write(s_out, span(c - 1, half), folded)

            @pl.when(z != mine)
            def _():
                swap(c).start()

        @pl.loop(0, c + 1)
        def _(t):
            done = p[c % slots, pl.ds(pl.multiple_of(t * tall, tall), tall), : 2 * tall]
            done = done.reshape(4, step, 2 * tall)
            for k in range(4):
                column = (k * chunks + c) * step
                o_ref[:, pl.ds(pl.multiple_of(t * step, step), step), column : column + step] = done[
                    :, :, k * step : (k + 1) * step
                ]

    def reflect(c):
        if not c:
            return

        @pl.when(z != mine)
        def _():
            swap(c).wait_recv()

        @pl.when(z == mine)
        def _():
            begin, size = span(c - 1, half)
            s_in[begin : begin + size + 16] = s_out[begin : begin + size + 16]

        got = read(s_in, span(c - 1, half))
        for back, part in ((0, got), (1, pltpu.roll(got, tall, 1))):
            turned = part.T[:tall].reshape(4, step, c * half)
            for q in range(c * half // step):
                row = back * c * half + q * step
                t, k = row // tall, row % tall // step
                column = (k * chunks + t) * step
                o_ref[:, c * step : (c + 1) * step, column : column + step] = turned[
                    :, :, q * step : (q + 1) * step
                ]

    for j in (1, 2, 3):
        e_copy(j, True).start()
    for c in range(ahead):
        start_z(c)
    for c in range(lead):
        start_own(c)
    local = pltpu.make_async_copy(x_ref.at[z], g.at[:, mine, z], ls)
    local.start()
    weigh()
    local.wait()
    for c in range(chunks + 4):
        if c < chunks:
            for j in (1, 2, 3):
                arrive(c, j)
            start_z(c + ahead)
            start_own(c + lead)
            scale(c)
        if 0 <= c - 1 < chunks:
            cross(c - 1)
            compute(c - 1)
        if 0 <= c - 2 < chunks:
            nearer(c - 2)
        if 0 <= c - 3 < chunks:
            finish(c - 3)
        if 0 <= c - 4 < chunks:
            reflect(c - 4)

    for j in (1, 2, 3):
        e_copy(j, True).wait_send()
    for c in range(chunks):
        near(c).wait_send()
        far(c).wait_send()
        for j in (1, 2, 3):
            z_copy(c, j, True).wait_send()
        for j in range(4):
            x_copy(c, j, True).wait_send()
            for k in range(2):
                c_copy(c, k, j, True).wait_send()

    @pl.when(z != mine)
    def _():
        for c in range(1, chunks):
            swap(c).wait_send()


def fused(pieces, eps_occ, eps_virt, freq):
    _, chunks, step, width = pieces.shape
    tall = 4 * step
    slots = 4
    sizes = (chunks, step, width, slots, 3, 4)
    total = chunks * (chunks + 1) // 2
    folded = total * tall // 2 + 16 * chunks
    dma = pltpu.SemaphoreType.DMA
    return pl.pallas_call(
        functools.partial(fused_kernel, sizes),
        out_shape=jax.ShapeDtypeStruct((4, chunks * step, chunks * tall), jnp.float32),
        in_specs=[
            pl.BlockSpec(memory_space=pl.ANY),
            pl.BlockSpec(memory_space=pltpu.SMEM),
            pl.BlockSpec(memory_space=pltpu.VMEM),
            pl.BlockSpec(memory_space=pltpu.SMEM),
        ],
        out_specs=pl.BlockSpec(memory_space=pltpu.VMEM),
        scratch_shapes=[
            pltpu.VMEM((chunks, 4, 4, step, width), jnp.bfloat16),
            pltpu.VMEM((chunks * tall, width), jnp.bfloat16),
            pltpu.VMEM((slots, chunks * tall, 4 * tall), jnp.float32),
            pltpu.VMEM((total * tall + 16 * chunks, 2 * tall), jnp.bfloat16),
            pltpu.VMEM((total * tall + 16 * chunks, 2 * tall), jnp.bfloat16),
            pltpu.VMEM((folded, 2 * tall), jnp.bfloat16),
            pltpu.VMEM((folded, 2 * tall), jnp.bfloat16),
            pltpu.VMEM((folded, 2 * tall), jnp.bfloat16),
            pltpu.VMEM((folded, 2 * tall), jnp.bfloat16),
            pltpu.VMEM((4, 1, width // 4), jnp.float32),
            pltpu.VMEM((1, width), jnp.float32),
            dma((chunks, 3)),
            dma((chunks, 3)),
            dma((chunks, 4)),
            dma((chunks, 4)),
            dma((chunks, 2, 4)),
            dma((chunks, 2, 4)),
            dma,
            dma((chunks,)),
            dma((chunks,)),
            dma((chunks,)),
            dma((chunks,)),
            dma((chunks,)),
            dma((chunks,)),
            dma((3,)),
            dma((3,)),
        ],
        compiler_params=pltpu.CompilerParams(
            collective_id=1, has_side_effects=True, vmem_limit_bytes=63 * 2**20
        ),
    )(pieces, eps_occ, eps_virt[None, :], freq)


def local(mesh, three_center, eps_occ, eps_virt, freq):
    n_pair, n_aux, n_rep = (mesh.shape[name] for name in ("pair", "aux", "rep"))
    rows, n_occ, n_virt = three_center.shape
    if n_pair == n_occ == 4 and n_aux == n_rep == 2 and rows % 16 == 0:
        return whole_kernel(three_center, eps_occ, eps_virt, freq)
    return staged(n_pair, n_aux, n_rep, three_center, eps_occ, eps_virt, freq)


def whole_kernel(three_center, eps_occ, eps_virt, freq):
    rows, n_pair, n_virt = three_center.shape
    pieces = three_center.transpose(1, 0, 2).reshape(n_pair, rows // 16, 16, n_virt)
    return fused(pieces, eps_occ, eps_virt, freq).reshape(n_pair * rows, n_pair * rows)


def staged(n_pair, n_aux, n_rep, three_center, eps_occ, eps_virt, freq):
    rows, n_occ, n_virt = three_center.shape
    parts = n_pair // n_occ
    width = n_virt // parts
    every_virt = lax.all_gather(eps_virt, "pair", axis=0, tiled=True)
    pieces = three_center.reshape(rows, n_pair, width).transpose(1, 0, 2)
    gathered = gather(pieces, n_aux, n_rep)

    z = lax.axis_index("pair")
    virt = lax.dynamic_slice_in_dim(every_virt, lax.rem(z, parts) * width, width)
    occ = lax.dynamic_index_in_dim(eps_occ, z // parts, keepdims=False)
    excite = virt - occ
    weight = 2.0 * excite / (excite * excite + freq[0] * freq[0])
    plain = gathered.reshape(n_aux * n_rep, n_pair * rows, width)
    mine = lax.axis_index("aux") * n_rep + lax.axis_index("rep")
    own = lax.dynamic_index_in_dim(plain, mine, keepdims=False)
    scaled = (own.astype(jnp.float32) * weight[None, :]).astype(jnp.bfloat16)
    partial_sums = lax.dot_general(
        scaled,
        plain.reshape(-1, width),
        (((1,), (1,)), ((), ())),
        preferred_element_type=jnp.float32,
    )
    return lax.psum_scatter(partial_sums, "pair", scatter_dimension=1, tiled=True)


def solution(mesh):
    return jax.shard_map(
        functools.partial(local, mesh),
        mesh=mesh,
        in_specs=(
            P(("grp", "aux", "rep", "pair"), None, None),
            P("grp"),
            P(("grp", "pair")),
            P("grp"),
        ),
        out_specs=P(("grp", "aux", "rep"), "pair"),
        check_vma=False,
    )
```

```python
import functools
import jax
import jax.numpy as jnp
from jax import lax
from jax.experimental import pallas as pl
from jax.experimental.pallas import tpu as pltpu
from jax.sharding import PartitionSpec as P

MESH = pl.DeviceIdType.MESH


def gather_kernel(sizes, x_ref, g_ref, zs, zr, xs, xr, cs, cr, ls):
    n_pair, n_aux, n_rep, chunks, rows = sizes
    z = lax.axis_index("pair")
    a = lax.axis_index("aux")
    r = lax.axis_index("rep")
    step = rows // chunks

    def turn(i, k, n):
        return lax.rem(i + k, n)

    peers = (
        [("pair", turn(z, k, n_pair)) for k in range(1, n_pair)]
        + [("aux", turn(a, k, n_aux)) for k in range(1, n_aux)]
        + [("rep", turn(r, k, n_rep)) for k in range(1, n_rep)]
    )
    barrier = pltpu.get_barrier_semaphore()
    for name, index in peers:
        pl.semaphore_signal(barrier, inc=1, device_id={name: index}, device_id_type=MESH)
    pl.semaphore_wait(barrier, len(peers))

    def block(aux, rep, pair, c):
        return g_ref.at[aux, rep, pair, pl.ds(c * step, step)]

    def z_copy(c, k, sending):
        to = turn(z, k, n_pair)
        src = turn(z, n_pair - k, n_pair)
        return pltpu.make_async_remote_copy(
            src_ref=x_ref.at[to, pl.ds(c * step, step)],
            dst_ref=block(a, r, z if sending else src, c),
            send_sem=zs.at[c, k],
            recv_sem=zr.at[c, k],
            device_id={"pair": to},
            device_id_type=MESH,
        )

    def x_copy(c, k, j, sending):
        pair = turn(z, n_pair - j, n_pair)
        mine = a if sending else turn(a, n_aux - k, n_aux)
        if j == 0 and sending:
            src = x_ref.at[z, pl.ds(c * step, step)]
        else:
            src = block(mine, r, pair, c)
        return pltpu.make_async_remote_copy(
            src_ref=src,
            dst_ref=block(mine, r, pair, c),
            send_sem=xs.at[c, k, j],
            recv_sem=xr.at[c, k, j],
            device_id={"aux": turn(a, k, n_aux)},
            device_id_type=MESH,
        )

    def c_copy(c, m, k, j, sending):
        pair = turn(z, n_pair - j, n_pair)
        aux = turn(a, n_aux - k, n_aux)
        rep = r if sending else turn(r, n_rep - m, n_rep)
        if j == 0 and k == 0 and sending:
            src = x_ref.at[z, pl.ds(c * step, step)]
        else:
            src = block(aux, rep, pair, c)
        return pltpu.make_async_remote_copy(
            src_ref=src,
            dst_ref=block(aux, rep, pair, c),
            send_sem=cs.at[c, m, k, j],
            recv_sem=cr.at[c, m, k, j],
            device_id={"rep": turn(r, m, n_rep)},
            device_id_type=MESH,
        )

    for c in range(chunks):
        for k in range(1, n_pair):
            z_copy(c, k, True).start()
    own = pltpu.make_async_copy(x_ref.at[z], g_ref.at[a, r, z], ls)
    own.start()

    def arrived(c, j):
        if j:
            z_copy(c, j, False).wait_recv()
        for k in range(1, n_aux):
            x_copy(c, k, j, True).start()
        for m in range(1, n_rep):
            c_copy(c, m, 0, j, True).start()

    def crossed(c, j):
        for k in range(1, n_aux):
            x_copy(c, k, j, False).wait_recv()
            for m in range(1, n_rep):
                c_copy(c, m, k, j, True).start()

    for c in range(chunks):
        arrived(c, 0)
    for c in range(chunks):
        for j in range(1, n_pair):
            arrived(c, j)
        crossed(c, 0)
        if c:
            for j in range(1, n_pair):
                crossed(c - 1, j)
    for j in range(1, n_pair):
        crossed(chunks - 1, j)

    own.wait()
    for c in range(chunks):
        for k in range(1, n_pair):
            z_copy(c, k, True).wait_send()
        for j in range(n_pair):
            for k in range(1, n_aux):
                x_copy(c, k, j, True).wait_send()
            for m in range(1, n_rep):
                for k in range(n_aux):
                    c_copy(c, m, k, j, True).wait_send()
                    c_copy(c, m, k, j, False).wait_recv()


def gather(pieces, n_aux, n_rep):
    n_pair, rows, width = pieces.shape
    chunks = 5 if rows % 80 == 0 else 1
    sizes = (n_pair, n_aux, n_rep, chunks, rows)
    dma = pltpu.SemaphoreType.DMA
    return pl.pallas_call(
        functools.partial(gather_kernel, sizes),
        out_shape=jax.ShapeDtypeStruct((n_aux, n_rep, n_pair, rows, width), pieces.dtype),
        in_specs=[pl.BlockSpec(memory_space=pl.ANY)],
        out_specs=pl.BlockSpec(memory_space=pl.ANY),
        scratch_shapes=[
            dma((chunks, n_pair)),
            dma((chunks, n_pair)),
            dma((chunks, n_aux, n_pair)),
            dma((chunks, n_aux, n_pair)),
            dma((chunks, n_rep, n_aux, n_pair)),
            dma((chunks, n_rep, n_aux, n_pair)),
            dma,
        ],
        compiler_params=pltpu.CompilerParams(collective_id=0, has_side_effects=True),
    )(pieces)


def encode(y):
    top = jnp.maximum(jnp.max(jnp.abs(y), axis=0, keepdims=True), 1e-30)
    scales = jnp.broadcast_to(top, (16, top.shape[1])).astype(jnp.bfloat16)
    power = jnp.abs(y) * (180.0 / scales[:1].astype(jnp.float32))
    for _ in range(4):
        power = power * power
    return jnp.where(y < 0, -power, power).astype(jnp.bfloat16), scales


def decode(code, scales):
    power = code.astype(jnp.float32)
    size = jnp.abs(power)
    root = jnp.maximum(size, 1e-37)
    for _ in range(4):
        root = lax.rsqrt(root)
    scale = scales[:1].astype(jnp.float32) * (1.0 / 180.0)
    return jnp.where(size < 1e-37, 0.0, jnp.where(power < 0, -root, root)) * scale


def fused_kernel(
    sizes, t_ref, occ_ref, virt_ref, freq_ref, o_ref, x_ref, g, own, p, n_out, n_in, f_out, f_in, s_out, s_in,
    raw, cut, levels, w_ref, zs, zr, xs, xr, cs, cr, rs, ls, ns, nr, fs, fr, ss, sr, es, er,
):
    chunks, step, width, slots, ahead, lead, lag = sizes
    z = lax.axis_index("pair")
    a = lax.axis_index("aux")
    r = lax.axis_index("rep")
    mine = 2 * a + r
    tall = 4 * step
    half = 2 * step
    flips = [z, z + 1 - 2 * lax.rem(z, 2), lax.rem(z + 2, 4), 3 - z]
    mirror = {"pair": mine, "aux": lax.div(z, 2), "rep": lax.rem(z, 2)}

    def load(c):
        rows = t_ref.at[c * step : (c + 1) * step]
        return pltpu.make_async_copy(rows, raw.at[c % 2], rs.at[c % 2])

    load(0).start()
    barrier = pltpu.get_barrier_semaphore()
    peers = [{"pair": flips[j]} for j in (1, 2, 3)] + [{"aux": 1 - a}, {"rep": 1 - r}]
    for peer in peers:
        pl.semaphore_signal(barrier, inc=1, device_id=peer, device_id_type=MESH)

    @pl.when(z != mine)
    def _():
        pl.semaphore_signal(barrier, inc=1, device_id=mirror, device_id_type=MESH)
        pl.semaphore_wait(barrier, len(peers) + 1)

    @pl.when(z == mine)
    def _():
        pl.semaphore_wait(barrier, len(peers))

    def send(src, dst, send_sem, recv_sem, to):
        return pltpu.make_async_remote_copy(
            src_ref=src, dst_ref=dst, send_sem=send_sem, recv_sem=recv_sem,
            device_id=to, device_id_type=MESH,
        )

    def z_copy(c, j, sending):
        dst = g.at[c, mine, z if sending else flips[j]]
        return send(x_ref.at[flips[j], c], dst, zs.at[c, j - 1], zr.at[c, j - 1], {"pair": flips[j]})

    def x_copy(c, j, sending):
        dst = g.at[c, 2 * (a if sending else 1 - a) + r, flips[j]]
        return send(dst, dst, xs.at[c, j], xr.at[c, j], {"aux": 1 - a})

    def c_copy(c, k, j, sending):
        aux = 1 - a if k else a
        dst = g.at[c, 2 * aux + (r if sending else 1 - r), flips[j]]
        return send(dst, dst, cs.at[c, k, j], cr.at[c, k, j], {"rep": 1 - r})

    def e_copy(j, sending):
        dst = levels.at[z if sending else flips[j]]
        return send(virt_ref, dst, es.at[j - 1], er.at[j - 1], {"pair": flips[j]})

    def span(c, unit):
        begin = unit * c * (c + 1) // 2 + 16 * c
        return begin, unit * (c + 1)

    def both(begin, size):
        return pl.ds(begin, size + 16)

    def near(c):
        rows = both(*span(c, tall))
        return send(n_out.at[rows], n_in.at[rows], ns.at[c], nr.at[c], {"pair": flips[1]})

    def far(c):
        rows = both(*span(c, half))
        return send(f_out.at[rows], f_in.at[rows], fs.at[c], fr.at[c], {"pair": flips[2]})

    def swap(c):
        rows = both(*span(c - 1, half))
        return send(s_out.at[rows], s_in.at[rows], ss.at[c], sr.at[c], mirror)

    def write(ref, where, y):
        begin, size = where
        ref[begin : begin + size], ref[begin + size : begin + size + 16] = encode(y)

    def read(ref, where):
        begin, size = where
        return decode(ref[begin : begin + size], ref[begin + size : begin + size + 16])

    def low(shape):
        return lax.broadcasted_iota(jnp.int32, shape, 1) < tall

    def start_z(c):
        if c < chunks:
            for j in (1, 2, 3):
                z_copy(c, j, True).start()

    def start_own(c):
        if c < chunks:
            load(c).wait()
            if c + 1 < chunks:
                load(c + 1).start()
            cut[...] = jnp.swapaxes(raw[c % 2], 0, 1)
            store = pltpu.make_async_copy(cut, x_ref.at[:, c], ls)
            store.start()
            g[c, mine, z] = cut[z]
            store.wait()
            x_copy(c, 0, True).start()
            c_copy(c, 0, 0, True).start()

    def arrive(c, j):
        z_copy(c, j, False).wait_recv()
        x_copy(c, j, True).start()
        c_copy(c, 0, j, True).start()

    def weigh():
        levels[z] = virt_ref[...]
        for j in (1, 2, 3):
            e_copy(j, False).wait_recv()
        freq = freq_ref[0]
        piece = virt_ref.shape[1]
        for k in range(4):
            excite = levels[k] - occ_ref[z]
            w_ref[:, k * piece : (k + 1) * piece] = 2.0 * excite / (excite * excite + freq * freq)

    def scale(c):
        plain = g[c, mine].reshape(tall, width).astype(jnp.float32)
        own[c * tall : (c + 1) * tall] = (plain * w_ref[...]).astype(jnp.bfloat16)

    def cross(c):
        for j in range(4):
            x_copy(c, j, False).wait_recv()
            c_copy(c, 1, j, True).start()
        for j in range(4):
            for k in range(2):
                c_copy(c, k, j, False).wait_recv()

    def compute(c):
        rows = (c + 1) * tall
        rhs = jnp.concatenate([g[c, flips[j]].reshape(tall, width) for j in (0, 2, 1, 3)], axis=0)
        p[c % slots, :rows] = lax.dot_general(
            own[:rows], rhs, (((1,), (1,)), ((), ())), preferred_element_type=jnp.float32
        )
        write(n_out, span(c, tall), p[c % slots, :rows, 2 * tall :])
        near(c).start()

    def nearer(c):
        rows = (c + 1) * tall
        near(c).wait_recv()
        p[c % slots, :rows, : 2 * tall] += read(n_in, span(c, tall))
        upper = p[c % slots, : rows // 2, : 2 * tall]
        lower = p[c % slots, rows // 2 : rows, : 2 * tall]
        folded = jnp.where(low(upper.shape), pltpu.roll(upper, tall, 1), lower)
        write(f_out, span(c, half), folded)
        far(c).start()

    def finish(c):
        rows = (c + 1) * tall
        far(c).wait_recv()
        got = read(f_in, span(c, half))
        p[c % slots, : rows // 2, : 2 * tall] += got
        p[c % slots, rows // 2 : rows, : 2 * tall] += pltpu.roll(got, tall, 1)
        if c:
            kept = c * half
            upper = p[c % slots, :kept, : 2 * tall]
            lower = p[c % slots, kept : 2 * kept, : 2 * tall]
            folded = jnp.where(low(upper.shape), upper, pltpu.roll(lower, tall, 1))
            write(s_out, span(c - 1, half), folded)

            @pl.when(z != mine)
            def _():
                swap(c).start()

        @pl.loop(0, c + 1)
        def _(t):
            done = p[c % slots, pl.ds(pl.multiple_of(t * tall, tall), tall), : 2 * tall]
            done = done.reshape(4, step, 2 * tall)
            for k in range(4):
                column = (k * chunks + c) * step
                o_ref[:, pl.ds(pl.multiple_of(t * step, step), step), column : column + step] = done[
                    :, :, k * step : (k + 1) * step
                ]

    def reflect(c):
        if not c:
            return

        @pl.when(z != mine)
        def _():
            swap(c).wait_recv()

        @pl.when(z == mine)
        def _():
            begin, size = span(c - 1, half)
            s_in[begin : begin + size + 16] = s_out[begin : begin + size + 16]

        got = read(s_in, span(c - 1, half))
        for back, part in ((0, got), (1, pltpu.roll(got, tall, 1))):
            turned = part.T[:tall].reshape(4, step, c * half)
            for q in range(c * half // step):
                row = back * c * half + q * step
                t, k = row // tall, row % tall // step
                column = (k * chunks + t) * step
                o_ref[:, c * step : (c + 1) * step, column : column + step] = turned[
                    :, :, q * step : (q + 1) * step
                ]

    for j in (1, 2, 3):
        e_copy(j, True).start()
    for c in range(lead):
        start_own(c)
        if c < ahead:
            start_z(c)
    weigh()
    todo = {nearer: 0, finish: 0, reflect: 0}

    def catch_up(stage, last):
        while todo[stage] <= last:
            stage(todo[stage])
            todo[stage] += 1

    for c in range(chunks):
        for j in (1, 2, 3):
            arrive(c, j)
            if c + ahead < chunks:
                z_copy(c + ahead, j, True).start()
        start_own(c + lead)
        scale(c)
        if c:
            cross(c - 1)
            compute(c - 1)
        catch_up(nearer, c - lag)
        catch_up(finish, c - lag - 1)
        catch_up(reflect, c - lag - 2)
    catch_up(nearer, chunks - 3)
    catch_up(finish, chunks - 5)
    cross(chunks - 1)
    compute(chunks - 1)
    catch_up(nearer, chunks - 2)
    catch_up(finish, chunks - 4)
    catch_up(nearer, chunks - 1)
    catch_up(finish, chunks - 2)
    catch_up(reflect, chunks - 4)
    catch_up(finish, chunks - 1)
    catch_up(reflect, chunks - 1)

    for j in (1, 2, 3):
        e_copy(j, True).wait_send()
    for c in range(chunks):
        near(c).wait_send()
        far(c).wait_send()
        for j in (1, 2, 3):
            z_copy(c, j, True).wait_send()
        for j in range(4):
            x_copy(c, j, True).wait_send()
            for k in range(2):
                c_copy(c, k, j, True).wait_send()

    @pl.when(z != mine)
    def _():
        for c in range(1, chunks):
            swap(c).wait_send()


def fused(three_center, eps_occ, eps_virt, freq):
    rows, _, width = three_center.shape
    step = 16
    chunks = rows // step
    tall = 4 * step
    slots = 4
    sizes = (chunks, step, width, slots, 1, 4, 3)
    total = chunks * (chunks + 1) // 2
    folded = total * tall // 2 + 16 * chunks
    dma = pltpu.SemaphoreType.DMA
    return pl.pallas_call(
        functools.partial(fused_kernel, sizes),
        out_shape=(
            jax.ShapeDtypeStruct((4, chunks * step, chunks * tall), jnp.float32),
            jax.ShapeDtypeStruct((4, chunks, step, width), three_center.dtype),
        ),
        in_specs=[
            pl.BlockSpec(memory_space=pl.ANY),
            pl.BlockSpec(memory_space=pltpu.SMEM),
            pl.BlockSpec(memory_space=pltpu.VMEM),
            pl.BlockSpec(memory_space=pltpu.SMEM),
        ],
        out_specs=(pl.BlockSpec(memory_space=pltpu.VMEM), pl.BlockSpec(memory_space=pl.ANY)),
        scratch_shapes=[
            pltpu.VMEM((chunks, 4, 4, step, width), jnp.bfloat16),
            pltpu.VMEM((chunks * tall, width), jnp.bfloat16),
            pltpu.VMEM((slots, chunks * tall, 4 * tall), jnp.float32),
            pltpu.VMEM((total * tall + 16 * chunks, 2 * tall), jnp.bfloat16),
            pltpu.VMEM((total * tall + 16 * chunks, 2 * tall), jnp.bfloat16),
            pltpu.VMEM((folded, 2 * tall), jnp.bfloat16),
            pltpu.VMEM((folded, 2 * tall), jnp.bfloat16),
            pltpu.VMEM((folded, 2 * tall), jnp.bfloat16),
            pltpu.VMEM((folded, 2 * tall), jnp.bfloat16),
            pltpu.VMEM((2, step, 4, width), jnp.bfloat16),
            pltpu.VMEM((4, step, width), jnp.bfloat16),
            pltpu.VMEM((4, 1, width // 4), jnp.float32),
            pltpu.VMEM((1, width), jnp.float32),
            dma((chunks, 3)),
            dma((chunks, 3)),
            dma((chunks, 4)),
            dma((chunks, 4)),
            dma((chunks, 2, 4)),
            dma((chunks, 2, 4)),
            dma((2,)),
            dma,
            dma((chunks,)),
            dma((chunks,)),
            dma((chunks,)),
            dma((chunks,)),
            dma((chunks,)),
            dma((chunks,)),
            dma((3,)),
            dma((3,)),
        ],
        compiler_params=pltpu.CompilerParams(
            collective_id=1, has_side_effects=True, vmem_limit_bytes=63 * 2**20
        ),
    )(three_center, eps_occ, eps_virt[None, :], freq)


def local(mesh, three_center, eps_occ, eps_virt, freq):
    n_pair, n_aux, n_rep = (mesh.shape[name] for name in ("pair", "aux", "rep"))
    rows, n_occ, n_virt = three_center.shape
    if n_pair == n_occ == 4 and n_aux == n_rep == 2 and rows % 16 == 0:
        return whole_kernel(three_center, eps_occ, eps_virt, freq)
    return staged(n_pair, n_aux, n_rep, three_center, eps_occ, eps_virt, freq)


def whole_kernel(three_center, eps_occ, eps_virt, freq):
    polar, _ = fused(three_center, eps_occ, eps_virt, freq)
    return polar.reshape(polar.shape[0] * polar.shape[1], polar.shape[2])


def staged(n_pair, n_aux, n_rep, three_center, eps_occ, eps_virt, freq):
    rows, n_occ, n_virt = three_center.shape
    parts = n_pair // n_occ
    width = n_virt // parts
    every_virt = lax.all_gather(eps_virt, "pair", axis=0, tiled=True)
    pieces = three_center.reshape(rows, n_pair, width).transpose(1, 0, 2)
    gathered = gather(pieces, n_aux, n_rep)

    z = lax.axis_index("pair")
    virt = lax.dynamic_slice_in_dim(every_virt, lax.rem(z, parts) * width, width)
    occ = lax.dynamic_index_in_dim(eps_occ, z // parts, keepdims=False)
    excite = virt - occ
    weight = 2.0 * excite / (excite * excite + freq[0] * freq[0])
    plain = gathered.reshape(n_aux * n_rep, n_pair * rows, width)
    mine = lax.axis_index("aux") * n_rep + lax.axis_index("rep")
    own = lax.dynamic_index_in_dim(plain, mine, keepdims=False)
    scaled = (own.astype(jnp.float32) * weight[None, :]).astype(jnp.bfloat16)
    partial_sums = lax.dot_general(
        scaled,
        plain.reshape(-1, width),
        (((1,), (1,)), ((), ())),
        preferred_element_type=jnp.float32,
    )
    return lax.psum_scatter(partial_sums, "pair", scatter_dimension=1, tiled=True)


def solution(mesh):
    return jax.shard_map(
        functools.partial(local, mesh),
        mesh=mesh,
        in_specs=(
            P(("grp", "aux", "rep", "pair"), None, None),
            P("grp"),
            P(("grp", "pair")),
            P("grp"),
        ),
        out_specs=P(("grp", "aux", "rep"), "pair"),
        check_vma=False,
    )
```

```python
import functools
import jax
import jax.numpy as jnp
from jax import lax
from jax.experimental import pallas as pl
from jax.experimental.pallas import tpu as pltpu
from jax.sharding import PartitionSpec as P

MESH = pl.DeviceIdType.MESH


def gather_kernel(sizes, x_ref, g_ref, zs, zr, xs, xr, cs, cr, ls):
    n_pair, n_aux, n_rep, chunks, rows = sizes
    z = lax.axis_index("pair")
    a = lax.axis_index("aux")
    r = lax.axis_index("rep")
    step = rows // chunks

    def turn(i, k, n):
        return lax.rem(i + k, n)

    peers = (
        [("pair", turn(z, k, n_pair)) for k in range(1, n_pair)]
        + [("aux", turn(a, k, n_aux)) for k in range(1, n_aux)]
        + [("rep", turn(r, k, n_rep)) for k in range(1, n_rep)]
    )
    barrier = pltpu.get_barrier_semaphore()
    for name, index in peers:
        pl.semaphore_signal(barrier, inc=1, device_id={name: index}, device_id_type=MESH)
    pl.semaphore_wait(barrier, len(peers))

    def block(aux, rep, pair, c):
        return g_ref.at[aux, rep, pair, pl.ds(c * step, step)]

    def z_copy(c, k, sending):
        to = turn(z, k, n_pair)
        src = turn(z, n_pair - k, n_pair)
        return pltpu.make_async_remote_copy(
            src_ref=x_ref.at[to, pl.ds(c * step, step)],
            dst_ref=block(a, r, z if sending else src, c),
            send_sem=zs.at[c, k],
            recv_sem=zr.at[c, k],
            device_id={"pair": to},
            device_id_type=MESH,
        )

    def x_copy(c, k, j, sending):
        pair = turn(z, n_pair - j, n_pair)
        mine = a if sending else turn(a, n_aux - k, n_aux)
        if j == 0 and sending:
            src = x_ref.at[z, pl.ds(c * step, step)]
        else:
            src = block(mine, r, pair, c)
        return pltpu.make_async_remote_copy(
            src_ref=src,
            dst_ref=block(mine, r, pair, c),
            send_sem=xs.at[c, k, j],
            recv_sem=xr.at[c, k, j],
            device_id={"aux": turn(a, k, n_aux)},
            device_id_type=MESH,
        )

    def c_copy(c, m, k, j, sending):
        pair = turn(z, n_pair - j, n_pair)
        aux = turn(a, n_aux - k, n_aux)
        rep = r if sending else turn(r, n_rep - m, n_rep)
        if j == 0 and k == 0 and sending:
            src = x_ref.at[z, pl.ds(c * step, step)]
        else:
            src = block(aux, rep, pair, c)
        return pltpu.make_async_remote_copy(
            src_ref=src,
            dst_ref=block(aux, rep, pair, c),
            send_sem=cs.at[c, m, k, j],
            recv_sem=cr.at[c, m, k, j],
            device_id={"rep": turn(r, m, n_rep)},
            device_id_type=MESH,
        )

    for c in range(chunks):
        for k in range(1, n_pair):
            z_copy(c, k, True).start()
    own = pltpu.make_async_copy(x_ref.at[z], g_ref.at[a, r, z], ls)
    own.start()

    def arrived(c, j):
        if j:
            z_copy(c, j, False).wait_recv()
        for k in range(1, n_aux):
            x_copy(c, k, j, True).start()
        for m in range(1, n_rep):
            c_copy(c, m, 0, j, True).start()

    def crossed(c, j):
        for k in range(1, n_aux):
            x_copy(c, k, j, False).wait_recv()
            for m in range(1, n_rep):
                c_copy(c, m, k, j, True).start()

    for c in range(chunks):
        arrived(c, 0)
    for c in range(chunks):
        for j in range(1, n_pair):
            arrived(c, j)
        crossed(c, 0)
        if c:
            for j in range(1, n_pair):
                crossed(c - 1, j)
    for j in range(1, n_pair):
        crossed(chunks - 1, j)

    own.wait()
    for c in range(chunks):
        for k in range(1, n_pair):
            z_copy(c, k, True).wait_send()
        for j in range(n_pair):
            for k in range(1, n_aux):
                x_copy(c, k, j, True).wait_send()
            for m in range(1, n_rep):
                for k in range(n_aux):
                    c_copy(c, m, k, j, True).wait_send()
                    c_copy(c, m, k, j, False).wait_recv()


def gather(pieces, n_aux, n_rep):
    n_pair, rows, width = pieces.shape
    chunks = 5 if rows % 80 == 0 else 1
    sizes = (n_pair, n_aux, n_rep, chunks, rows)
    dma = pltpu.SemaphoreType.DMA
    return pl.pallas_call(
        functools.partial(gather_kernel, sizes),
        out_shape=jax.ShapeDtypeStruct((n_aux, n_rep, n_pair, rows, width), pieces.dtype),
        in_specs=[pl.BlockSpec(memory_space=pl.ANY)],
        out_specs=pl.BlockSpec(memory_space=pl.ANY),
        scratch_shapes=[
            dma((chunks, n_pair)),
            dma((chunks, n_pair)),
            dma((chunks, n_aux, n_pair)),
            dma((chunks, n_aux, n_pair)),
            dma((chunks, n_rep, n_aux, n_pair)),
            dma((chunks, n_rep, n_aux, n_pair)),
            dma,
        ],
        compiler_params=pltpu.CompilerParams(collective_id=0, has_side_effects=True),
    )(pieces)


def encode(y):
    top = jnp.maximum(jnp.max(jnp.abs(y), axis=0, keepdims=True), 1e-30)
    scales = jnp.broadcast_to(top, (16, top.shape[1])).astype(jnp.bfloat16)
    power = jnp.abs(y) * (180.0 / scales[:1].astype(jnp.float32))
    for _ in range(4):
        power = power * power
    return jnp.where(y < 0, -power, power).astype(jnp.bfloat16), scales


def decode(code, scales):
    power = code.astype(jnp.float32)
    size = jnp.abs(power)
    root = jnp.maximum(size, 1e-37)
    for _ in range(4):
        root = lax.rsqrt(root)
    scale = scales[:1].astype(jnp.float32) * (1.0 / 180.0)
    return jnp.where(size < 1e-37, 0.0, jnp.where(power < 0, -root, root)) * scale


def fused_kernel(
    sizes, t_ref, occ_ref, virt_ref, freq_ref, o_ref, x_ref, g, own, p, n_out, n_in, f_out, f_in, s_out, s_in, via,
    raw, cut, levels, w_ref, zs, zr, xs, xr, cs, cr, rs, ls, ns, nr, fs, fr, ss, sr, hs, hr, es, er,
):
    chunks, step, width, slots, ahead, lead, lag, parts, detour_parts = sizes
    z = lax.axis_index("pair")
    a = lax.axis_index("aux")
    r = lax.axis_index("rep")
    mine = 2 * a + r
    tall = 4 * step
    half = 2 * step
    flips = [z, z + 1 - 2 * lax.rem(z, 2), lax.rem(z + 2, 4), 3 - z]
    mirror = {"pair": mine, "aux": lax.div(z, 2), "rep": lax.rem(z, 2)}
    across = lax.div(z, 2) != a
    beyond = {"pair": 3 - 2 * a, "aux": a, "rep": lax.rem(z, 2)}
    helper = {"pair": mine, "aux": a, "rep": 1}
    detours = across & (r == 1)
    relays = jnp.logical_not(across) & (r == 1)
    relayed = across & (lax.rem(z, 2) == 1)

    def load(c):
        rows = t_ref.at[c * step : (c + 1) * step]
        return pltpu.make_async_copy(rows, raw.at[c % 2], rs.at[c % 2])

    load(0).start()
    barrier = pltpu.get_barrier_semaphore()
    peers = [{"pair": flips[j]} for j in (1, 2, 3)] + [{"aux": 1 - a}, {"rep": 1 - r}]
    for peer in peers:
        pl.semaphore_signal(barrier, inc=1, device_id=peer, device_id_type=MESH)

    @pl.when(z != mine)
    def _():
        pl.semaphore_signal(barrier, inc=1, device_id=mirror, device_id_type=MESH)

    @pl.when(relayed)
    def _():
        pl.semaphore_signal(barrier, inc=1, device_id=helper, device_id_type=MESH)

    extra = (z != mine).astype(jnp.int32) + relays.astype(jnp.int32)
    pl.semaphore_wait(barrier, len(peers) + extra)

    def send(src, dst, send_sem, recv_sem, to):
        return pltpu.make_async_remote_copy(
            src_ref=src, dst_ref=dst, send_sem=send_sem, recv_sem=recv_sem,
            device_id=to, device_id_type=MESH,
        )

    def z_copy(c, j, sending):
        dst = g.at[c, mine, z if sending else flips[j]]
        return send(x_ref.at[flips[j], c], dst, zs.at[c, j - 1], zr.at[c, j - 1], {"pair": flips[j]})

    def x_copy(c, j, sending):
        dst = g.at[c, 2 * (a if sending else 1 - a) + r, flips[j]]
        return send(dst, dst, xs.at[c, j], xr.at[c, j], {"aux": 1 - a})

    def c_copy(c, k, j, sending):
        aux = 1 - a if k else a
        dst = g.at[c, 2 * aux + (r if sending else 1 - r), flips[j]]
        return send(dst, dst, cs.at[c, k, j], cr.at[c, k, j], {"rep": 1 - r})

    def e_copy(j, sending):
        dst = levels.at[z if sending else flips[j]]
        return send(virt_ref, dst, es.at[j - 1], er.at[j - 1], {"pair": flips[j]})

    def lay(counts):
        begins = [sum(counts[:i]) + 16 * i for i in range(len(counts))]
        return list(zip(begins, counts))

    near_rows = lay([count for _, _, count in parts])
    far_rows = lay([count // 2 for _, _, count in parts])
    kept = [min(begin + count, c * tall) - begin for c, begin, count in parts]
    swap_rows = lay([count // 2 for count in kept])

    def both(where):
        return pl.ds(where[0], where[1] + 16)

    def near(i):
        rows = both(near_rows[i])
        return send(n_out.at[rows], n_in.at[rows], ns.at[i], nr.at[i], {"pair": flips[1]})

    def far(i):
        rows = both(far_rows[i])
        return send(f_out.at[rows], f_in.at[rows], fs.at[i], fr.at[i], {"pair": flips[2]})

    def swap(i):
        rows = both(swap_rows[i])
        return send(s_out.at[rows], s_in.at[rows], ss.at[i], sr.at[i], mirror)

    def lend(i):
        rows = both(swap_rows[i])
        return send(s_out.at[rows], via.at[rows], ss.at[i], hr.at[i], {"aux": 1 - a})

    def forward(i):
        rows = both(swap_rows[i])
        return send(via.at[rows], s_in.at[rows], hs.at[i], sr.at[i], beyond)

    def write(ref, where, y):
        begin, size = where
        ref[begin : begin + size], ref[begin + size : begin + size + 16] = encode(y)

    def read(ref, where):
        begin, size = where
        return decode(ref[begin : begin + size], ref[begin + size : begin + size + 16])

    def low(shape):
        return lax.broadcasted_iota(jnp.int32, shape, 1) < tall

    waiting = [(c, j) for c in range(chunks) for j in (1, 2, 3)]

    def start_z(count):
        for _ in range(min(count, len(waiting))):
            z_copy(*waiting.pop(0), True).start()

    def start_own(c):
        if c < chunks:
            load(c).wait()
            if c + 1 < chunks:
                load(c + 1).start()
            cut[...] = jnp.swapaxes(raw[c % 2], 0, 1)
            store = pltpu.make_async_copy(cut, x_ref.at[:, c], ls)
            store.start()
            g[c, mine, z] = cut[z]
            store.wait()
            x_copy(c, 0, True).start()
            c_copy(c, 0, 0, True).start()

    def arrive(c, j):
        z_copy(c, j, False).wait_recv()
        x_copy(c, j, True).start()
        c_copy(c, 0, j, True).start()

    def weigh():
        levels[z] = virt_ref[...]
        for j in (1, 2, 3):
            e_copy(j, False).wait_recv()
        freq = freq_ref[0]
        piece = virt_ref.shape[1]
        for k in range(4):
            excite = levels[k] - occ_ref[z]
            w_ref[:, k * piece : (k + 1) * piece] = 2.0 * excite / (excite * excite + freq * freq)

    def scale(c):
        plain = g[c, mine].reshape(tall, width).astype(jnp.float32)
        own[c * tall : (c + 1) * tall] = (plain * w_ref[...]).astype(jnp.bfloat16)

    def cross(c):
        for j in range(4):
            x_copy(c, j, False).wait_recv()
            c_copy(c, 1, j, True).start()
        for j in range(4):
            for k in range(2):
                c_copy(c, k, j, False).wait_recv()

    def compute(i):
        c, begin, count = parts[i]
        rows = pl.ds(begin, count)
        rhs = jnp.concatenate([g[c, flips[j]].reshape(tall, width) for j in (0, 2, 1, 3)], axis=0)
        p[c % slots, rows] = lax.dot_general(
            own[rows], rhs, (((1,), (1,)), ((), ())), preferred_element_type=jnp.float32
        )
        write(n_out, near_rows[i], p[c % slots, rows, 2 * tall :])
        near(i).start()

    def nearer(i):
        c, begin, count = parts[i]
        near(i).wait_recv()
        p[c % slots, pl.ds(begin, count), : 2 * tall] += read(n_in, near_rows[i])
        upper = p[c % slots, pl.ds(begin, count // 2), : 2 * tall]
        lower = p[c % slots, pl.ds(begin + count // 2, count // 2), : 2 * tall]
        write(f_out, far_rows[i], jnp.where(low(upper.shape), pltpu.roll(upper, tall, 1), lower))
        far(i).start()

    def finish(i):
        c, begin, count = parts[i]
        far(i).wait_recv()
        got = read(f_in, far_rows[i])
        p[c % slots, pl.ds(begin, count // 2), : 2 * tall] += got
        p[c % slots, pl.ds(begin + count // 2, count // 2), : 2 * tall] += pltpu.roll(got, tall, 1)
        if kept[i]:
            size = kept[i] // 2
            upper = p[c % slots, pl.ds(begin, size), : 2 * tall]
            lower = p[c % slots, pl.ds(begin + size, size), : 2 * tall]
            write(s_out, swap_rows[i], jnp.where(low(upper.shape), upper, pltpu.roll(lower, tall, 1)))

            if i < detour_parts:
                @pl.when(detours)
                def _():
                    lend(i).start()

                @pl.when((z != mine) & jnp.logical_not(detours))
                def _():
                    swap(i).start()
            else:
                @pl.when(z != mine)
                def _():
                    swap(i).start()

        @pl.loop(0, count // step // 4)
        def _(n):
            t = begin // tall + n
            done = p[c % slots, pl.ds(pl.multiple_of(t * tall, tall), tall), : 2 * tall]
            done = done.reshape(4, step, 2 * tall)
            for k in range(4):
                column = (k * chunks + c) * step
                o_ref[:, pl.ds(pl.multiple_of(t * step, step), step), column : column + step] = done[
                    :, :, k * step : (k + 1) * step
                ]

    def pass_on(i):
        if kept[i] and i < detour_parts:
            @pl.when(relays)
            def _():
                lend(i).wait_recv()
                forward(i).start()

    def reflect(i):
        c, begin, count = parts[i]
        if not kept[i]:
            return

        @pl.when(z != mine)
        def _():
            swap(i).wait_recv()

        @pl.when(z == mine)
        def _():
            rows = both(swap_rows[i])
            s_in[rows] = s_out[rows]

        size = kept[i] // 2
        got = read(s_in, swap_rows[i])
        for back, part in ((0, got), (1, pltpu.roll(got, tall, 1))):
            turned = part.T[:tall].reshape(4, step, size)
            for q in range(size // step):
                row = begin + back * size + q * step
                t, k = row // tall, row % tall // step
                column = (k * chunks + t) * step
                o_ref[:, c * step : (c + 1) * step, column : column + step] = turned[
                    :, :, q * step : (q + 1) * step
                ]

    def settle(c):
        for j in (1, 2, 3):
            z_copy(c, j, True).wait_send()
        for j in range(4):
            x_copy(c, j, True).wait_send()
            for k in range(2):
                c_copy(c, k, j, True).wait_send()

    for j in (1, 2, 3):
        e_copy(j, True).start()
    for c in range(lead):
        start_own(c)
        if c == 0:
            start_z(3)
        if c == 1:
            start_z(ahead)
    weigh()
    todo = {nearer: 0, finish: 0, pass_on: 0, reflect: 0, settle: 0}

    def catch_up(stage, last):
        while todo[stage] <= last:
            stage(todo[stage])
            todo[stage] += 1

    for c in range(chunks):
        for j in (1, 2, 3):
            arrive(c, j)
            start_z(1)
        start_own(c + lead)
        scale(c)
        if c:
            cross(c - 1)
            compute(c - 1)
        catch_up(nearer, c - lag)
        catch_up(finish, c - lag - 1)
        catch_up(pass_on, c - lag - 2)
        catch_up(reflect, c - lag - 3)
        catch_up(settle, c - 3)
    last = chunks - 1
    catch_up(nearer, last - 2)
    catch_up(finish, last - 4)
    catch_up(settle, last - 2)
    cross(last)
    for i in range(last, len(parts)):
        compute(i)
    catch_up(nearer, last - 1)
    catch_up(nearer, last)
    catch_up(finish, last - 3)
    catch_up(pass_on, last - 3)
    catch_up(nearer, len(parts) - 1)
    catch_up(finish, last - 1)
    catch_up(finish, last)
    catch_up(pass_on, len(parts) - 1)
    catch_up(reflect, last - 3)
    catch_up(finish, len(parts) - 1)
    catch_up(settle, last)
    catch_up(reflect, len(parts) - 1)

    for j in (1, 2, 3):
        e_copy(j, True).wait_send()
    for i in range(len(parts)):
        near(i).wait_send()
        far(i).wait_send()

    @pl.when(z != mine)
    def _():
        for i in range(len(parts)):
            if kept[i]:
                swap(i).wait_send()

    @pl.when(relays)
    def _():
        for i in range(detour_parts):
            if kept[i]:
                forward(i).wait_send()


def fused(three_center, eps_occ, eps_virt, freq):
    rows, _, width = three_center.shape
    step = 16
    chunks = rows // step
    tall = 4 * step
    slots = 4
    splits = 2 if chunks > 1 else 1
    whole = [(c, 0, (c + 1) * tall) for c in range(chunks - 1)]
    portion = chunks * tall // splits
    parts = whole + [(chunks - 1, i * portion, portion) for i in range(splits)]
    sizes = (chunks, step, width, slots, 1, 4, 3, parts, chunks - 1)
    near_size = chunks * (chunks + 1) // 2 * tall + 16 * len(parts)
    far_size = near_size // 2 + 8 * len(parts)
    dma = pltpu.SemaphoreType.DMA
    return pl.pallas_call(
        functools.partial(fused_kernel, sizes),
        out_shape=(
            jax.ShapeDtypeStruct((4, chunks * step, chunks * tall), jnp.float32),
            jax.ShapeDtypeStruct((4, chunks, step, width), three_center.dtype),
        ),
        in_specs=[
            pl.BlockSpec(memory_space=pl.ANY),
            pl.BlockSpec(memory_space=pltpu.SMEM),
            pl.BlockSpec(memory_space=pltpu.VMEM),
            pl.BlockSpec(memory_space=pltpu.SMEM),
        ],
        out_specs=(pl.BlockSpec(memory_space=pltpu.VMEM), pl.BlockSpec(memory_space=pl.ANY)),
        scratch_shapes=[
            pltpu.VMEM((chunks, 4, 4, step, width), jnp.bfloat16),
            pltpu.VMEM((chunks * tall, width), jnp.bfloat16),
            pltpu.VMEM((slots, chunks * tall, 4 * tall), jnp.float32),
            pltpu.VMEM((near_size, 2 * tall), jnp.bfloat16),
            pltpu.VMEM((near_size, 2 * tall), jnp.bfloat16),
            pltpu.VMEM((far_size, 2 * tall), jnp.bfloat16),
            pltpu.VMEM((far_size, 2 * tall), jnp.bfloat16),
            pltpu.VMEM((far_size, 2 * tall), jnp.bfloat16),
            pltpu.VMEM((far_size, 2 * tall), jnp.bfloat16),
            pltpu.VMEM((far_size, 2 * tall), jnp.bfloat16),
            pltpu.VMEM((2, step, 4, width), jnp.bfloat16),
            pltpu.VMEM((4, step, width), jnp.bfloat16),
            pltpu.VMEM((4, 1, width // 4), jnp.float32),
            pltpu.VMEM((1, width), jnp.float32),
            dma((chunks, 3)),
            dma((chunks, 3)),
            dma((chunks, 4)),
            dma((chunks, 4)),
            dma((chunks, 2, 4)),
            dma((chunks, 2, 4)),
            dma((2,)),
            dma,
            dma((len(parts),)),
            dma((len(parts),)),
            dma((len(parts),)),
            dma((len(parts),)),
            dma((len(parts),)),
            dma((len(parts),)),
            dma((len(parts),)),
            dma((len(parts),)),
            dma((3,)),
            dma((3,)),
        ],
        compiler_params=pltpu.CompilerParams(
            collective_id=1, has_side_effects=True, vmem_limit_bytes=63 * 2**20
        ),
    )(three_center, eps_occ, eps_virt[None, :], freq)


def local(mesh, three_center, eps_occ, eps_virt, freq):
    n_pair, n_aux, n_rep = (mesh.shape[name] for name in ("pair", "aux", "rep"))
    rows, n_occ, n_virt = three_center.shape
    if n_pair == n_occ == 4 and n_aux == n_rep == 2 and rows % 16 == 0:
        return whole_kernel(three_center, eps_occ, eps_virt, freq)
    return staged(n_pair, n_aux, n_rep, three_center, eps_occ, eps_virt, freq)


def whole_kernel(three_center, eps_occ, eps_virt, freq):
    polar, _ = fused(three_center, eps_occ, eps_virt, freq)
    return polar.reshape(polar.shape[0] * polar.shape[1], polar.shape[2])


def staged(n_pair, n_aux, n_rep, three_center, eps_occ, eps_virt, freq):
    rows, n_occ, n_virt = three_center.shape
    parts = n_pair // n_occ
    width = n_virt // parts
    every_virt = lax.all_gather(eps_virt, "pair", axis=0, tiled=True)
    pieces = three_center.reshape(rows, n_pair, width).transpose(1, 0, 2)
    gathered = gather(pieces, n_aux, n_rep)

    z = lax.axis_index("pair")
    virt = lax.dynamic_slice_in_dim(every_virt, lax.rem(z, parts) * width, width)
    occ = lax.dynamic_index_in_dim(eps_occ, z // parts, keepdims=False)
    excite = virt - occ
    weight = 2.0 * excite / (excite * excite + freq[0] * freq[0])
    plain = gathered.reshape(n_aux * n_rep, n_pair * rows, width)
    mine = lax.axis_index("aux") * n_rep + lax.axis_index("rep")
    own = lax.dynamic_index_in_dim(plain, mine, keepdims=False)
    scaled = (own.astype(jnp.float32) * weight[None, :]).astype(jnp.bfloat16)
    partial_sums = lax.dot_general(
        scaled,
        plain.reshape(-1, width),
        (((1,), (1,)), ((), ())),
        preferred_element_type=jnp.float32,
    )
    return lax.psum_scatter(partial_sums, "pair", scatter_dimension=1, tiled=True)


def solution(mesh):
    return jax.shard_map(
        functools.partial(local, mesh),
        mesh=mesh,
        in_specs=(
            P(("grp", "aux", "rep", "pair"), None, None),
            P("grp"),
            P(("grp", "pair")),
            P("grp"),
        ),
        out_specs=P(("grp", "aux", "rep"), "pair"),
        check_vma=False,
    )
```

```python
import functools
import jax
import jax.numpy as jnp
from jax import lax
from jax.experimental import pallas as pl
from jax.experimental.pallas import tpu as pltpu
from jax.sharding import PartitionSpec as P

MESH = pl.DeviceIdType.MESH


def gather_kernel(sizes, x_ref, g_ref, zs, zr, xs, xr, cs, cr, ls):
    n_pair, n_aux, n_rep, chunks, rows = sizes
    z = lax.axis_index("pair")
    a = lax.axis_index("aux")
    r = lax.axis_index("rep")
    step = rows // chunks

    def turn(i, k, n):
        return lax.rem(i + k, n)

    peers = (
        [("pair", turn(z, k, n_pair)) for k in range(1, n_pair)]
        + [("aux", turn(a, k, n_aux)) for k in range(1, n_aux)]
        + [("rep", turn(r, k, n_rep)) for k in range(1, n_rep)]
    )
    barrier = pltpu.get_barrier_semaphore()
    for name, index in peers:
        pl.semaphore_signal(barrier, inc=1, device_id={name: index}, device_id_type=MESH)
    pl.semaphore_wait(barrier, len(peers))

    def block(aux, rep, pair, c):
        return g_ref.at[aux, rep, pair, pl.ds(c * step, step)]

    def z_copy(c, k, sending):
        to = turn(z, k, n_pair)
        src = turn(z, n_pair - k, n_pair)
        return pltpu.make_async_remote_copy(
            src_ref=x_ref.at[to, pl.ds(c * step, step)],
            dst_ref=block(a, r, z if sending else src, c),
            send_sem=zs.at[c, k],
            recv_sem=zr.at[c, k],
            device_id={"pair": to},
            device_id_type=MESH,
        )

    def x_copy(c, k, j, sending):
        pair = turn(z, n_pair - j, n_pair)
        mine = a if sending else turn(a, n_aux - k, n_aux)
        if j == 0 and sending:
            src = x_ref.at[z, pl.ds(c * step, step)]
        else:
            src = block(mine, r, pair, c)
        return pltpu.make_async_remote_copy(
            src_ref=src,
            dst_ref=block(mine, r, pair, c),
            send_sem=xs.at[c, k, j],
            recv_sem=xr.at[c, k, j],
            device_id={"aux": turn(a, k, n_aux)},
            device_id_type=MESH,
        )

    def c_copy(c, m, k, j, sending):
        pair = turn(z, n_pair - j, n_pair)
        aux = turn(a, n_aux - k, n_aux)
        rep = r if sending else turn(r, n_rep - m, n_rep)
        if j == 0 and k == 0 and sending:
            src = x_ref.at[z, pl.ds(c * step, step)]
        else:
            src = block(aux, rep, pair, c)
        return pltpu.make_async_remote_copy(
            src_ref=src,
            dst_ref=block(aux, rep, pair, c),
            send_sem=cs.at[c, m, k, j],
            recv_sem=cr.at[c, m, k, j],
            device_id={"rep": turn(r, m, n_rep)},
            device_id_type=MESH,
        )

    for c in range(chunks):
        for k in range(1, n_pair):
            z_copy(c, k, True).start()
    own = pltpu.make_async_copy(x_ref.at[z], g_ref.at[a, r, z], ls)
    own.start()

    def arrived(c, j):
        if j:
            z_copy(c, j, False).wait_recv()
        for k in range(1, n_aux):
            x_copy(c, k, j, True).start()
        for m in range(1, n_rep):
            c_copy(c, m, 0, j, True).start()

    def crossed(c, j):
        for k in range(1, n_aux):
            x_copy(c, k, j, False).wait_recv()
            for m in range(1, n_rep):
                c_copy(c, m, k, j, True).start()

    for c in range(chunks):
        arrived(c, 0)
    for c in range(chunks):
        for j in range(1, n_pair):
            arrived(c, j)
        crossed(c, 0)
        if c:
            for j in range(1, n_pair):
                crossed(c - 1, j)
    for j in range(1, n_pair):
        crossed(chunks - 1, j)

    own.wait()
    for c in range(chunks):
        for k in range(1, n_pair):
            z_copy(c, k, True).wait_send()
        for j in range(n_pair):
            for k in range(1, n_aux):
                x_copy(c, k, j, True).wait_send()
            for m in range(1, n_rep):
                for k in range(n_aux):
                    c_copy(c, m, k, j, True).wait_send()
                    c_copy(c, m, k, j, False).wait_recv()


def gather(pieces, n_aux, n_rep):
    n_pair, rows, width = pieces.shape
    chunks = 5 if rows % 80 == 0 else 1
    sizes = (n_pair, n_aux, n_rep, chunks, rows)
    dma = pltpu.SemaphoreType.DMA
    return pl.pallas_call(
        functools.partial(gather_kernel, sizes),
        out_shape=jax.ShapeDtypeStruct((n_aux, n_rep, n_pair, rows, width), pieces.dtype),
        in_specs=[pl.BlockSpec(memory_space=pl.ANY)],
        out_specs=pl.BlockSpec(memory_space=pl.ANY),
        scratch_shapes=[
            dma((chunks, n_pair)),
            dma((chunks, n_pair)),
            dma((chunks, n_aux, n_pair)),
            dma((chunks, n_aux, n_pair)),
            dma((chunks, n_rep, n_aux, n_pair)),
            dma((chunks, n_rep, n_aux, n_pair)),
            dma,
        ],
        compiler_params=pltpu.CompilerParams(collective_id=0, has_side_effects=True),
    )(pieces)


def encode(y):
    top = jnp.maximum(jnp.max(jnp.abs(y), axis=0, keepdims=True), 1e-30)
    scales = jnp.broadcast_to(top, (16, top.shape[1])).astype(jnp.bfloat16)
    power = jnp.abs(y) * (180.0 / scales[:1].astype(jnp.float32))
    for _ in range(4):
        power = power * power
    return jnp.where(y < 0, -power, power).astype(jnp.bfloat16), scales


def decode(code, scales):
    power = code.astype(jnp.float32)
    size = jnp.abs(power)
    root = jnp.maximum(size, 1e-37)
    for _ in range(4):
        root = lax.rsqrt(root)
    scale = scales[:1].astype(jnp.float32) * (1.0 / 180.0)
    return jnp.where(size < 1e-37, 0.0, jnp.where(power < 0, -root, root)) * scale


def fused_kernel(
    sizes, t_ref, occ_ref, virt_ref, freq_ref, o_ref, x_ref, g, own, p, n_out, n_in, f_out, f_in, s_out, s_in, via,
    raw, cut, levels, w_ref, zs, zr, xs, xr, cs, cr, rs, ls, ns, nr, fs, fr, ss, sr, hs, hr, es, er,
):
    chunks, step, width, slots, ahead, lead, lag, parts, detour_parts = sizes
    z = lax.axis_index("pair")
    a = lax.axis_index("aux")
    r = lax.axis_index("rep")
    mine = 2 * a + r
    tall = 4 * step
    half = 2 * step
    flips = [z, z + 1 - 2 * lax.rem(z, 2), lax.rem(z + 2, 4), 3 - z]
    mirror = {"pair": mine, "aux": lax.div(z, 2), "rep": lax.rem(z, 2)}
    across = lax.div(z, 2) != a
    beyond = {"pair": 3 - 2 * a, "aux": a, "rep": lax.rem(z, 2)}
    helper = {"pair": mine, "aux": a, "rep": 1}
    detours = across & (r == 1)
    relays = jnp.logical_not(across) & (r == 1)
    relayed = across & (lax.rem(z, 2) == 1)

    def load(c):
        rows = t_ref.at[c * step : (c + 1) * step]
        return pltpu.make_async_copy(rows, raw.at[c % 2], rs.at[c % 2])

    load(0).start()
    barrier = pltpu.get_barrier_semaphore()
    peers = [{"pair": flips[j]} for j in (1, 2, 3)] + [{"aux": 1 - a}, {"rep": 1 - r}]
    for peer in peers:
        pl.semaphore_signal(barrier, inc=1, device_id=peer, device_id_type=MESH)

    @pl.when(z != mine)
    def _():
        pl.semaphore_signal(barrier, inc=1, device_id=mirror, device_id_type=MESH)

    @pl.when(relayed)
    def _():
        pl.semaphore_signal(barrier, inc=1, device_id=helper, device_id_type=MESH)

    extra = (z != mine).astype(jnp.int32) + relays.astype(jnp.int32)
    pl.semaphore_wait(barrier, len(peers) + extra)

    def send(src, dst, send_sem, recv_sem, to):
        return pltpu.make_async_remote_copy(
            src_ref=src, dst_ref=dst, send_sem=send_sem, recv_sem=recv_sem,
            device_id=to, device_id_type=MESH,
        )

    cut_at = width // 256 * 128

    def columns(ref, c):
        if c < chunks - 1:
            return ref
        return ref.at[:, :cut_at] if c < chunks else ref.at[:, cut_at:]

    def z_copy(c, j, sending):
        chunk = min(c, chunks - 1)
        dst = columns(g.at[chunk, mine, z if sending else flips[j]], c)
        return send(columns(x_ref.at[flips[j], chunk], c), dst, zs.at[c, j - 1], zr.at[c, j - 1], {"pair": flips[j]})

    def x_copy(c, j, sending):
        chunk = min(c, chunks - 1)
        dst = columns(g.at[chunk, 2 * (a if sending else 1 - a) + r, flips[j]], c)
        return send(dst, dst, xs.at[c, j], xr.at[c, j], {"aux": 1 - a})

    def c_copy(c, k, j, sending):
        aux = 1 - a if k else a
        chunk = min(c, chunks - 1)
        dst = columns(g.at[chunk, 2 * aux + (r if sending else 1 - r), flips[j]], c)
        return send(dst, dst, cs.at[c, k, j], cr.at[c, k, j], {"rep": 1 - r})

    def e_copy(j, sending):
        dst = levels.at[z if sending else flips[j]]
        return send(virt_ref, dst, es.at[j - 1], er.at[j - 1], {"pair": flips[j]})

    def lay(counts):
        begins = [sum(counts[:i]) + 16 * i for i in range(len(counts))]
        return list(zip(begins, counts))

    near_rows = lay([count for _, _, count in parts])
    far_rows = lay([count // 2 for _, _, count in parts])
    kept = [min(begin + count, c * tall) - begin for c, begin, count in parts]
    swap_rows = lay([count // 2 for count in kept])

    def both(where):
        return pl.ds(where[0], where[1] + 16)

    def near(i):
        rows = both(near_rows[i])
        return send(n_out.at[rows], n_in.at[rows], ns.at[i], nr.at[i], {"pair": flips[1]})

    def far(i):
        rows = both(far_rows[i])
        return send(f_out.at[rows], f_in.at[rows], fs.at[i], fr.at[i], {"pair": flips[2]})

    def swap(i):
        rows = both(swap_rows[i])
        return send(s_out.at[rows], s_in.at[rows], ss.at[i], sr.at[i], mirror)

    def lend(i):
        rows = both(swap_rows[i])
        return send(s_out.at[rows], via.at[rows], ss.at[i], hr.at[i], {"aux": 1 - a})

    def forward(i):
        rows = both(swap_rows[i])
        return send(via.at[rows], s_in.at[rows], hs.at[i], sr.at[i], beyond)

    def write(ref, where, y):
        begin, size = where
        ref[begin : begin + size], ref[begin + size : begin + size + 16] = encode(y)

    def read(ref, where):
        begin, size = where
        return decode(ref[begin : begin + size], ref[begin + size : begin + size + 16])

    def low(shape):
        return lax.broadcasted_iota(jnp.int32, shape, 1) < tall

    waiting = [(c, j) for c in range(chunks + 1) for j in (1, 2, 3)]

    def pieces(c):
        return (c,) if c < chunks - 1 else (c, c + 1)

    def start_z(count):
        for _ in range(min(count, len(waiting))):
            z_copy(*waiting.pop(0), True).start()

    def start_own(c):
        if c < chunks:
            load(c).wait()
            if c + 1 < chunks:
                load(c + 1).start()
            cut[...] = jnp.swapaxes(raw[c % 2], 0, 1)
            store = pltpu.make_async_copy(cut, x_ref.at[:, c], ls)
            store.start()
            g[c, mine, z] = cut[z]
            store.wait()
            for u in pieces(c):
                x_copy(u, 0, True).start()
                c_copy(u, 0, 0, True).start()

    def arrive(c, j):
        z_copy(c, j, False).wait_recv()
        x_copy(c, j, True).start()
        c_copy(c, 0, j, True).start()

    def weigh():
        levels[z] = virt_ref[...]
        for j in (1, 2, 3):
            e_copy(j, False).wait_recv()
        freq = freq_ref[0]
        piece = virt_ref.shape[1]
        for k in range(4):
            excite = levels[k] - occ_ref[z]
            w_ref[:, k * piece : (k + 1) * piece] = 2.0 * excite / (excite * excite + freq * freq)

    def scale(c):
        plain = g[c, mine].reshape(tall, width).astype(jnp.float32)
        own[c * tall : (c + 1) * tall] = (plain * w_ref[...]).astype(jnp.bfloat16)

    def cross(c):
        for u in pieces(c):
            for j in range(4):
                x_copy(u, j, False).wait_recv()
                c_copy(u, 1, j, True).start()
        for u in pieces(c):
            for j in range(4):
                for k in range(2):
                    c_copy(u, k, j, False).wait_recv()

    def compute(i):
        c, begin, count = parts[i]
        rows = pl.ds(begin, count)
        rhs = jnp.concatenate([g[c, flips[j]].reshape(tall, width) for j in (0, 2, 1, 3)], axis=0)
        p[c % slots, rows] = lax.dot_general(
            own[rows], rhs, (((1,), (1,)), ((), ())), preferred_element_type=jnp.float32
        )
        write(n_out, near_rows[i], p[c % slots, rows, 2 * tall :])
        near(i).start()

    def nearer(i):
        c, begin, count = parts[i]
        near(i).wait_recv()
        p[c % slots, pl.ds(begin, count), : 2 * tall] += read(n_in, near_rows[i])
        upper = p[c % slots, pl.ds(begin, count // 2), : 2 * tall]
        lower = p[c % slots, pl.ds(begin + count // 2, count // 2), : 2 * tall]
        write(f_out, far_rows[i], jnp.where(low(upper.shape), pltpu.roll(upper, tall, 1), lower))
        far(i).start()

    def finish(i):
        c, begin, count = parts[i]
        far(i).wait_recv()
        got = read(f_in, far_rows[i])
        p[c % slots, pl.ds(begin, count // 2), : 2 * tall] += got
        p[c % slots, pl.ds(begin + count // 2, count // 2), : 2 * tall] += pltpu.roll(got, tall, 1)
        if kept[i]:
            size = kept[i] // 2
            upper = p[c % slots, pl.ds(begin, size), : 2 * tall]
            lower = p[c % slots, pl.ds(begin + size, size), : 2 * tall]
            write(s_out, swap_rows[i], jnp.where(low(upper.shape), upper, pltpu.roll(lower, tall, 1)))

            if i < detour_parts:
                @pl.when(detours)
                def _():
                    lend(i).start()

                @pl.when((z != mine) & jnp.logical_not(detours))
                def _():
                    swap(i).start()
            else:
                @pl.when(z != mine)
                def _():
                    swap(i).start()

        @pl.loop(0, count // step // 4)
        def _(n):
            t = begin // tall + n
            done = p[c % slots, pl.ds(pl.multiple_of(t * tall, tall), tall), : 2 * tall]
            done = done.reshape(4, step, 2 * tall)
            for k in range(4):
                column = (k * chunks + c) * step
                o_ref[:, pl.ds(pl.multiple_of(t * step, step), step), column : column + step] = done[
                    :, :, k * step : (k + 1) * step
                ]

    def pass_on(i):
        if kept[i] and i < detour_parts:
            @pl.when(relays)
            def _():
                lend(i).wait_recv()
                forward(i).start()

    def reflect(i):
        c, begin, count = parts[i]
        if not kept[i]:
            return

        @pl.when(z != mine)
        def _():
            swap(i).wait_recv()

        @pl.when(z == mine)
        def _():
            rows = both(swap_rows[i])
            s_in[rows] = s_out[rows]

        size = kept[i] // 2
        got = read(s_in, swap_rows[i])
        for back, part in ((0, got), (1, pltpu.roll(got, tall, 1))):
            turned = part.T[:tall].reshape(4, step, size)
            for q in range(size // step):
                row = begin + back * size + q * step
                t, k = row // tall, row % tall // step
                column = (k * chunks + t) * step
                o_ref[:, c * step : (c + 1) * step, column : column + step] = turned[
                    :, :, q * step : (q + 1) * step
                ]

    def settle(c):
        for u in pieces(c):
            for j in (1, 2, 3):
                z_copy(u, j, True).wait_send()
            for j in range(4):
                x_copy(u, j, True).wait_send()
                for k in range(2):
                    c_copy(u, k, j, True).wait_send()

    for j in (1, 2, 3):
        e_copy(j, True).start()
    for c in range(lead):
        start_own(c)
        if c == 0:
            start_z(3)
        if c == 1:
            start_z(ahead)
    weigh()
    todo = {nearer: 0, finish: 0, pass_on: 0, reflect: 0, settle: 0}

    def catch_up(stage, last):
        while todo[stage] <= last:
            stage(todo[stage])
            todo[stage] += 1

    for c in range(chunks):
        for u in pieces(c):
            for j in (1, 2, 3):
                arrive(u, j)
                start_z(1)
        start_own(c + lead)
        scale(c)
        if c:
            cross(c - 1)
            compute(c - 1)
        catch_up(nearer, c - lag)
        catch_up(finish, c - lag - 1)
        catch_up(pass_on, c - lag - 2)
        catch_up(reflect, c - lag - 3)
        catch_up(settle, c - 3)
    last = chunks - 1
    catch_up(nearer, last - 2)
    catch_up(finish, last - 4)
    catch_up(settle, last - 2)
    cross(last)
    for i in range(last, len(parts)):
        compute(i)
    catch_up(nearer, last - 1)
    catch_up(nearer, last)
    catch_up(finish, last - 3)
    catch_up(pass_on, last - 3)
    catch_up(nearer, len(parts) - 1)
    catch_up(finish, last - 1)
    catch_up(finish, last)
    catch_up(pass_on, len(parts) - 1)
    catch_up(reflect, last - 3)
    catch_up(finish, len(parts) - 1)
    catch_up(settle, last)
    catch_up(reflect, len(parts) - 1)

    for j in (1, 2, 3):
        e_copy(j, True).wait_send()
    for i in range(len(parts)):
        near(i).wait_send()
        far(i).wait_send()

    @pl.when(z != mine)
    def _():
        for i in range(len(parts)):
            if kept[i]:
                swap(i).wait_send()

    @pl.when(relays)
    def _():
        for i in range(detour_parts):
            if kept[i]:
                forward(i).wait_send()


def fused(three_center, eps_occ, eps_virt, freq):
    rows, _, width = three_center.shape
    step = 16
    chunks = rows // step
    tall = 4 * step
    slots = 4
    splits = 2 if chunks > 1 else 1
    whole = [(c, 0, (c + 1) * tall) for c in range(chunks - 1)]
    portion = chunks * tall // splits
    parts = whole + [(chunks - 1, i * portion, portion) for i in range(splits)]
    sizes = (chunks, step, width, slots, 2, 3, 3, parts, chunks - 1)
    near_size = chunks * (chunks + 1) // 2 * tall + 16 * len(parts)
    far_size = near_size // 2 + 8 * len(parts)
    dma = pltpu.SemaphoreType.DMA
    return pl.pallas_call(
        functools.partial(fused_kernel, sizes),
        out_shape=(
            jax.ShapeDtypeStruct((4, chunks * step, chunks * tall), jnp.float32),
            jax.ShapeDtypeStruct((4, chunks, step, width), three_center.dtype),
        ),
        in_specs=[
            pl.BlockSpec(memory_space=pl.ANY),
            pl.BlockSpec(memory_space=pltpu.SMEM),
            pl.BlockSpec(memory_space=pltpu.VMEM),
            pl.BlockSpec(memory_space=pltpu.SMEM),
        ],
        out_specs=(pl.BlockSpec(memory_space=pltpu.VMEM), pl.BlockSpec(memory_space=pl.ANY)),
        scratch_shapes=[
            pltpu.VMEM((chunks, 4, 4, step, width), jnp.bfloat16),
            pltpu.VMEM((chunks * tall, width), jnp.bfloat16),
            pltpu.VMEM((slots, chunks * tall, 4 * tall), jnp.float32),
            pltpu.VMEM((near_size, 2 * tall), jnp.bfloat16),
            pltpu.VMEM((near_size, 2 * tall), jnp.bfloat16),
            pltpu.VMEM((far_size, 2 * tall), jnp.bfloat16),
            pltpu.VMEM((far_size, 2 * tall), jnp.bfloat16),
            pltpu.VMEM((far_size, 2 * tall), jnp.bfloat16),
            pltpu.VMEM((far_size, 2 * tall), jnp.bfloat16),
            pltpu.VMEM((far_size, 2 * tall), jnp.bfloat16),
            pltpu.VMEM((2, step, 4, width), jnp.bfloat16),
            pltpu.VMEM((4, step, width), jnp.bfloat16),
            pltpu.VMEM((4, 1, width // 4), jnp.float32),
            pltpu.VMEM((1, width), jnp.float32),
            dma((chunks + 1, 3)),
            dma((chunks + 1, 3)),
            dma((chunks + 1, 4)),
            dma((chunks + 1, 4)),
            dma((chunks + 1, 2, 4)),
            dma((chunks + 1, 2, 4)),
            dma((2,)),
            dma,
            dma((len(parts),)),
            dma((len(parts),)),
            dma((len(parts),)),
            dma((len(parts),)),
            dma((len(parts),)),
            dma((len(parts),)),
            dma((len(parts),)),
            dma((len(parts),)),
            dma((3,)),
            dma((3,)),
        ],
        compiler_params=pltpu.CompilerParams(
            collective_id=1, has_side_effects=True, vmem_limit_bytes=63 * 2**20
        ),
    )(three_center, eps_occ, eps_virt[None, :], freq)


def local(mesh, three_center, eps_occ, eps_virt, freq):
    n_pair, n_aux, n_rep = (mesh.shape[name] for name in ("pair", "aux", "rep"))
    rows, n_occ, n_virt = three_center.shape
    if n_pair == n_occ == 4 and n_aux == n_rep == 2 and rows % 16 == 0:
        return whole_kernel(three_center, eps_occ, eps_virt, freq)
    return staged(n_pair, n_aux, n_rep, three_center, eps_occ, eps_virt, freq)


def whole_kernel(three_center, eps_occ, eps_virt, freq):
    polar, _ = fused(three_center, eps_occ, eps_virt, freq)
    return polar.reshape(polar.shape[0] * polar.shape[1], polar.shape[2])


def staged(n_pair, n_aux, n_rep, three_center, eps_occ, eps_virt, freq):
    rows, n_occ, n_virt = three_center.shape
    parts = n_pair // n_occ
    width = n_virt // parts
    every_virt = lax.all_gather(eps_virt, "pair", axis=0, tiled=True)
    pieces = three_center.reshape(rows, n_pair, width).transpose(1, 0, 2)
    gathered = gather(pieces, n_aux, n_rep)

    z = lax.axis_index("pair")
    virt = lax.dynamic_slice_in_dim(every_virt, lax.rem(z, parts) * width, width)
    occ = lax.dynamic_index_in_dim(eps_occ, z // parts, keepdims=False)
    excite = virt - occ
    weight = 2.0 * excite / (excite * excite + freq[0] * freq[0])
    plain = gathered.reshape(n_aux * n_rep, n_pair * rows, width)
    mine = lax.axis_index("aux") * n_rep + lax.axis_index("rep")
    own = lax.dynamic_index_in_dim(plain, mine, keepdims=False)
    scaled = (own.astype(jnp.float32) * weight[None, :]).astype(jnp.bfloat16)
    partial_sums = lax.dot_general(
        scaled,
        plain.reshape(-1, width),
        (((1,), (1,)), ((), ())),
        preferred_element_type=jnp.float32,
    )
    return lax.psum_scatter(partial_sums, "pair", scatter_dimension=1, tiled=True)


def solution(mesh):
    return jax.shard_map(
        functools.partial(local, mesh),
        mesh=mesh,
        in_specs=(
            P(("grp", "aux", "rep", "pair"), None, None),
            P("grp"),
            P(("grp", "pair")),
            P("grp"),
        ),
        out_specs=P(("grp", "aux", "rep"), "pair"),
        check_vma=False,
    )
```
